32 devices in a mesh: dp: 4 (over y, x), tensor: 8 (over z, core).
Axes of the slice: x: 2, y: 2, z: 4, core: 2. Of those that a mesh axis runs over, the one named last changes fastest.
Arguments:
- hidden_act: bfloat16 [2816, 36864], P('dp', 'tensor'), may hold values from -80 to 80
- out_grad: bfloat16 [2816, 4608], P('dp', 'tensor'), may hold values from -0.5 to 0.5
- other_sq: float32 [8], P('dp'), may hold values from 2989699 to 597939968
Outputs:
- weight_grad: float32 [4608, 36864], P('dp', 'tensor')
The draws below stay inside these ranges and needn't reach their ends.
All inputs are finite; a program needn't handle non-finite values.
Results may differ from the reference program's by a relative error of at most 0.002.
Values may be sent and summed in bfloat16 or wider, within the bound.
No kernel may reach another device: no remote copies, remote signals or barrier semaphores. Data moves between devices by JAX's collectives and lax.ppermute only.
A program may use at most 128 MiB of HBM per device.

```python
import math
import jax
import jax.numpy as jnp
from jax import lax

D = 4608
FF = 36864
L = 352
EX_DEV = 2
EXAMPLES = 8
TOKENS = 2816
N_DP = 4


def draw_hidden_act(key, part):
    base_key = jax.random.fold_in(key, 11)
    noise_key = jax.random.fold_in(base_key, 0)
    column_key = jax.random.fold_in(base_key, 1)
    share_key = jax.random.fold_in(base_key, 3)
    factor_key = jax.random.fold_in(base_key, 4)
    values = jax.random.truncated_normal(noise_key, -3.0, 3.0, (EXAMPLES, L, FF), jnp.float32)
    ramp = 3.0 ** (jnp.arange(FF, dtype=jnp.float32) / FF)
    column_scale = ramp * jax.random.uniform(column_key, (FF,), jnp.float32, 0.5, 1.5)
    share_ratio = 0.85 / math.sqrt(L)
    direction = jax.random.truncated_normal(share_key, -3.0, 3.0, (EXAMPLES, 1, FF), jnp.float32) * math.sqrt(share_ratio)
    factor = jnp.exp(jax.random.uniform(factor_key, (EXAMPLES, L, 1), jnp.float32, math.log(0.5), math.log(2.0)))
    values = (values + factor * direction) * column_scale[None, None, :]
    values = values.reshape(TOKENS, FF)
    return jnp.clip(values, -80.0, 80.0).astype(jnp.bfloat16)


def draw_out_grad(key, part):
    base_key = jax.random.fold_in(key, 23)
    noise_key, share_key, factor_key, pair_key = jax.random.split(base_key, 4)
    sigma = 0.02
    share_ratio = 0.85 / math.sqrt(L)
    noise = jax.random.truncated_normal(noise_key, -4.0, 4.0, (EXAMPLES, L, D), jnp.float32) * sigma
    direction = jax.random.truncated_normal(share_key, -3.0, 3.0, (EXAMPLES, 1, D), jnp.float32) * (sigma * math.sqrt(share_ratio))
    factor = jnp.exp(jax.random.uniform(factor_key, (EXAMPLES, L, 1), jnp.float32, math.log(0.5), math.log(2.0)))
    values = (noise + factor * direction).reshape(TOKENS, D)
    groups = EXAMPLES // EX_DEV
    target = jax.random.permutation(pair_key, groups)
    row_group = jnp.arange(TOKENS, dtype=jnp.int32) // (EX_DEV * L)
    column_group = jnp.arange(D, dtype=jnp.int32) // (D // groups)
    paired = target[row_group][:, None] == column_group[None, :]
    values = values * jnp.where(paired, 3.0, 1.0)
    return jnp.clip(values, -0.5, 0.5).astype(jnp.bfloat16)


def steps_of(stream_key, dims, pieces, low, largest):
    def one(dim, shards_of):
        heights = jax.random.uniform(jax.random.fold_in(jax.random.fold_in(stream_key, 6), dim), (shards_of,), jnp.float32, low / len(pieces), largest / len(pieces))
        return jnp.repeat(jnp.exp(heights), dims[dim] // shards_of).reshape((-1,) + (1,) * (len(dims) - dim - 1))

    level = one(*pieces[0])
    for cut in pieces[1:]:
        level = level * one(*cut)
    return level


def setup_inputs(seed: int = 0) -> dict:
    key_list = jax.random.split(jax.random.key(seed), 4)
    return {
        "hidden_act": draw_hidden_act(jax.random.fold_in(key_list[3], 71), 0),
        "out_grad": draw_out_grad(jax.random.fold_in(key_list[3], 71), 0),
        "other_sq": jnp.clip(jnp.exp(math.log(597939968) - 5.2983176 * jax.random.uniform(key_list[2], (EXAMPLES,), jnp.float32) ** steps_of(key_list[2], (EXAMPLES,), ((0, 4),), -0.2, 0.2)), 2989699, 597939968),
    }


def reference(hidden_act, out_grad, other_sq):
    acts = hidden_act.astype(jnp.float32).reshape(EXAMPLES, L, FF)
    grads = out_grad.astype(jnp.float32).reshape(EXAMPLES, L, D)
    act_gram = jnp.einsum('etf,esf->ets', acts, acts, precision=lax.Precision.HIGHEST)
    grad_gram = jnp.einsum('etd,esd->ets', grads, grads, precision=lax.Precision.HIGHEST)
    layer_sq = lax.optimization_barrier(jnp.sum(act_gram * grad_gram, axis=(1, 2)))
    clip_bound = math.sqrt(L * FF * D / 80.0)
    clip_scale = jnp.minimum(1.0, clip_bound / jnp.sqrt(other_sq + layer_sq))
    scaled_grad = (grads * clip_scale[:, None, None]).astype(jnp.bfloat16).reshape(TOKENS, D)
    group_rows = EX_DEV * L
    running = jnp.zeros((D, FF), jnp.float32)
    for group in range(N_DP):
        columns = scaled_grad[group * group_rows:(group + 1) * group_rows].astype(jnp.float32)
        activations = hidden_act[group * group_rows:(group + 1) * group_rows].astype(jnp.float32)
        running = running + jnp.dot(columns.T, activations, precision=lax.Precision.HIGHEST)
    return running
```

```python
import functools
import math

import jax
import jax.numpy as jnp
from jax import lax
from jax.experimental import pallas as pl
from jax.experimental.pallas import tpu as pltpu
from jax.sharding import PartitionSpec as P

BF16, F32 = jnp.bfloat16, jnp.float32
CLIP_DIVISOR = 80.0


def bits_of(mask):
    return [1 << i for i in range(mask.bit_length()) if mask >> i & 1]


def swap(x, axis, size, mask):
    return lax.ppermute(x, axis, [(i, i ^ mask) for i in range(size)])


def chunk_widths(total):
    widths, start = [], 0
    for width, keep in ((768, 1536), (512, 512), (256, 0), (128, 0)):
        while total - start - width >= keep and start % width == 0:
            widths.append((start, width))
            start += width
    if start < total:
        widths = [(0, total)]
    return widths


def row_block(rows):
    for block in (288, 192, 144, 128, 96, 64, 48, 32, 16, 8):
        if rows % block == 0:
            return block
    return rows


def matmul_kernel(n_dp, n_in, *refs):
    grad_ref, act_refs, out_ref = refs[0], refs[1 : 1 + n_dp], refs[n_in]
    total = jnp.dot(grad_ref[0], act_refs[0][...], preferred_element_type=F32)
    for s in range(1, n_dp):
        total += jnp.dot(grad_ref[s], act_refs[s][...], preferred_element_type=F32)
    out_ref[...] = total


def chunk_matmul(grads, acts, out, start, width, out_shape):
    n_dp, rows, tokens = grads.shape
    block = row_block(rows)
    at = start // width
    specs = [pl.BlockSpec((n_dp, block, tokens), lambda i: (0, i, 0))]
    for array, whole in acts:
        specs.append(
            pl.BlockSpec((tokens, width), (lambda i: (0, at)) if whole else (lambda i: (0, 0)))
        )
    args = [grads] + [a for a, _ in acts]
    aliases = {}
    if out is not None:
        specs.append(pl.BlockSpec(memory_space=pl.ANY))
        args.append(out)
        aliases = {len(args) - 1: 0}
    return pl.pallas_call(
        functools.partial(matmul_kernel, n_dp, len(args)),
        grid=(rows // block,),
        in_specs=specs,
        out_specs=pl.BlockSpec((block, width), lambda i: (i, at)),
        out_shape=jax.ShapeDtypeStruct(out_shape, F32),
        input_output_aliases=aliases,
        cost_estimate=pl.CostEstimate(
            flops=2 * rows * width * n_dp * tokens,
            bytes_accessed=2 * n_dp * tokens * (rows + width) + 4 * rows * width,
            transcendentals=0,
        ),
        name="chunk_matmul",
    )(*args)


def prepare_kernel(n, where_ref, scale_ref, *refs):
    pieces, out_ref = refs[:n], refs[n]
    step = pl.program_id(0)
    scale = scale_ref[...]
    for k in range(n):

        @pl.when(step == k)
        def _(k=k):
            piece = pieces[k][...]
            out_ref[...] = (piece.astype(F32) * scale[:, None, None, :]).astype(BF16)[:, :, None]


def prepare(pieces, where, scale):
    n = len(pieces)
    groups, halves, rows, tokens = pieces[0].shape
    whole = pl.BlockSpec((groups, halves, rows, tokens), lambda k, w: (0, 0, 0, 0))
    return pl.pallas_call(
        functools.partial(prepare_kernel, n),
        grid_spec=pltpu.PrefetchScalarGridSpec(
            num_scalar_prefetch=1,
            grid=(n,),
            in_specs=[pl.BlockSpec((groups, tokens), lambda k, w: (0, 0))] + [whole] * n,
            out_specs=pl.BlockSpec(
                (groups, halves, 1, rows, tokens), lambda k, w: (0, 0, w[k], 0, 0)
            ),
        ),
        out_shape=jax.ShapeDtypeStruct((groups, halves, n, rows, tokens), BF16),
        cost_estimate=pl.CostEstimate(
            flops=groups * halves * n * rows * tokens,
            bytes_accessed=4 * groups * halves * n * rows * tokens,
            transcendentals=0,
        ),
        name="prepare",
    )(where, scale, *pieces)


def on_device(n_dp, n_tensor, hidden_act, out_grad, other_sq):
    examples = other_sq.shape[0]
    tokens, columns = hidden_act.shape
    features = out_grad.shape[1]
    length = tokens // examples
    chips = n_tensor // 2
    me = lax.axis_index("dp")
    place = lax.axis_index("tensor")

    blocks = {1 << i: None for i in range(n_dp.bit_length() - 1)}
    for mask in blocks:
        blocks[mask] = swap(hidden_act, "dp", n_dp, mask)

    grad = out_grad.T
    share = features // n_tensor
    spread = lax.all_to_all(
        grad.reshape(n_tensor, share, tokens), "tensor", split_axis=0, concat_axis=0, tiled=True
    )
    halves = n_tensor // n_dp
    spread = spread.reshape(n_dp, halves, share, tokens)
    mine = [
        lax.dynamic_index_in_dim(spread, me ^ s, 0, keepdims=False) for s in range(n_dp)
    ]
    piece = jnp.stack([mine[0]] + [swap(mine[s], "dp", n_dp, s) for s in range(1, n_dp)])
    ring = [(i, (i + 2) % n_tensor) for i in range(n_tensor)]
    pieces, where = [], []
    for k in range(chips):
        if k:
            piece = lax.ppermute(piece, "tensor", ring)
        origin = (place // 2 - k) % chips * 2
        pieces += [piece, swap(piece, "tensor", n_tensor, 1)]
        where += [origin + place % 2, origin + (place + 1) % 2]

    acts = hidden_act.reshape(examples, length, columns)
    act_gram = jnp.einsum("etf,esf->ets", acts, acts, preferred_element_type=F32)
    grads = grad.reshape(features, examples, length)
    grad_gram = jnp.einsum("fet,fes->ets", grads, grads, preferred_element_type=F32)
    grams = jnp.stack([act_gram.reshape(tokens, length), grad_gram.reshape(tokens, length)])
    rows, first = tokens, 0
    mask = 1
    while mask < n_tensor:
        rows //= 2
        bit = (place // mask) % 2
        sent = lax.dynamic_slice_in_dim(grams, (1 - bit) * rows, rows, 1)
        kept = lax.dynamic_slice_in_dim(grams, bit * rows, rows, 1)
        grams = kept + swap(sent, "tensor", n_tensor, mask)
        first = first + bit * rows
        mask *= 2
    row_sum = jnp.sum(grams[0] * grams[1], axis=1)
    example = (first + jnp.arange(rows, dtype=jnp.int32)) // length
    layer_sq = jnp.sum(
        jnp.where(example[None] == jnp.arange(examples, dtype=jnp.int32)[:, None], row_sum[None], 0.0),
        axis=1,
    )
    mask = 1
    while mask < n_tensor:
        layer_sq = layer_sq + swap(layer_sq, "tensor", n_tensor, mask)
        mask *= 2
    total_columns, total_features = columns * n_tensor, features * n_tensor
    clip_bound = math.sqrt(length * total_columns * total_features / CLIP_DIVISOR)
    clip_scale = jnp.minimum(1.0, clip_bound / jnp.sqrt(other_sq + layer_sq))
    scales = jnp.stack([clip_scale] + [swap(clip_scale, "dp", n_dp, s) for s in range(1, n_dp)])
    token_scale = jnp.broadcast_to(scales[:, :, None], (n_dp, examples, length)).reshape(n_dp, tokens)
    scaled = prepare(pieces, jnp.stack(where).astype(jnp.int32), token_scale)
    scaled = scaled.reshape(n_dp, halves * n_tensor * share, tokens)

    out = None
    out_shape = (scaled.shape[1], columns)
    for c, (start, width) in enumerate(chunk_widths(columns)):
        parts = {0: (hidden_act, True)}
        for mask, block in blocks.items():
            parts[mask] = (block, True)
        for mask in sorted(range(1, n_dp), key=lambda m: len(bits_of(m))):
            bits = bits_of(mask)
            if len(bits) == 1:
                continue
            bit = bits[c % len(bits)]
            source, whole = parts[mask ^ bit]
            if whole:
                source = lax.slice_in_dim(source, start, start + width, axis=1)
            parts[mask] = (swap(source, "dp", n_dp, bit), False)
        out = chunk_matmul(scaled, [parts[s] for s in range(n_dp)], out, start, width, out_shape)
    return out


def solution(mesh):
    placed = (P("dp", "tensor"), P("dp", "tensor"), P("dp"))
    body = functools.partial(on_device, mesh.shape["dp"], mesh.shape["tensor"])
    return jax.shard_map(
        body, mesh=mesh, in_specs=placed, out_specs=P("dp", "tensor"), check_vma=False
    )
```

```python
import functools
import math

import jax
import jax.numpy as jnp
from jax import lax
from jax.experimental import pallas as pl
from jax.experimental.pallas import tpu as pltpu
from jax.sharding import PartitionSpec as P


BF16, F32 = jnp.bfloat16, jnp.float32
CLIP_DIVISOR = 80.0
VMEM_LIMIT = 57 << 20
NEAR_SHARES = (2, 3, 2, 2)
CHUNK_SHARES = (2, 3, 2, 1, 1)


def bits_of(mask):
    return [1 << i for i in range(mask.bit_length()) if mask >> i & 1]


def swap(x, axis, size, mask):
    return lax.ppermute(x, axis, [(i, i ^ mask) for i in range(size)])


def after(*arrays):
    return lax.optimization_barrier(arrays)


def cut(total, shares):
    if total % (2 * sum(shares)):
        shares = (1,)
    unit, start, pieces = total // sum(shares), 0, []
    for share in shares:
        pieces.append((start, share * unit))
        start += share * unit
    return pieces


def row_block(rows):
    for block in (288, 192, 144, 128, 96, 64, 48, 32, 16, 8):
        if rows % block == 0:
            return block
    return rows


def matmul_kernel(terms, block, tiles, adds, *refs):
    grad_ref, out_ref, refs = refs[0], refs[-1], refs[1:]

    def multiply(side):
        for at in range(0, out_ref.shape[0], block):
            here = pl.ds(at, block)
            total, k = (refs[-2][here, :] if adds else None), 0
            for s, arrays in terms:
                act_ref = refs[k + side % arrays]
                k += arrays
                product = jnp.dot(grad_ref[s, here, :], act_ref[...], preferred_element_type=F32)
                total = product if total is None else total + product
            out_ref[here, :] = total

    if any(arrays > 1 for _, arrays in terms):
        step = pl.program_id(0)
        pl.when(step < tiles)(lambda: multiply(0))
        pl.when(step >= tiles)(lambda: multiply(1))
    else:
        multiply(0)


def chunk_matmul(grads, acts, out, start, width, adds, out_shape):
    _, rows, tokens = grads.shape
    tile = math.gcd(width // 2, 256)
    tiles = width // 2 // tile
    specs, args, terms = [pl.BlockSpec(memory_space=pltpu.VMEM)], [grads], []
    args = [pltpu.with_memory_space_constraint(grads, pltpu.VMEM)]
    for s, (array, other) in acts.items():
        if isinstance(other, int):
            maps = [(array, lambda j, at=other // tile: (0, at + j))]
        else:
            maps = [
                (array, lambda j: (0, jnp.minimum(j, tiles - 1))),
                (other, lambda j: (0, jnp.maximum(j - tiles, 0))),
            ]
        for array, index in maps:
            args.append(array)
            specs.append(pl.BlockSpec((tokens, tile), index))
        terms.append((s, len(maps)))
    window = pl.BlockSpec((rows, tile), lambda j: (0, start // tile + j))
    aliases = {}
    if out is not None:
        specs.append(window if adds else pl.BlockSpec(memory_space=pl.ANY))
        args.append(out)
        aliases = {len(args) - 1: 0}
    return pl.pallas_call(
        functools.partial(matmul_kernel, terms, row_block(rows), tiles, adds),
        grid=(2 * tiles,),
        in_specs=specs,
        out_specs=window,
        out_shape=jax.ShapeDtypeStruct(out_shape, F32),
        input_output_aliases=aliases,
        compiler_params=pltpu.CompilerParams(vmem_limit_bytes=VMEM_LIMIT),
        cost_estimate=pl.CostEstimate(
            flops=2 * rows * width * len(terms) * tokens,
            bytes_accessed=2 * len(terms) * tokens * width + 4 * rows * width * (1 + adds),
            transcendentals=0,
        ),
        name="chunk_matmul",
    )(*args)


def prepare_kernel(n, where_ref, scale_ref, *refs):
    pieces, out_ref = refs[:n], refs[n]
    step = pl.program_id(0)
    scale = scale_ref[...]
    for k in range(n):

        @pl.when(step == k)
        def _(k=k):
            piece = pieces[k][...]
            out_ref[...] = (piece.astype(F32) * scale[:, None, None, :]).astype(BF16)[:, :, None]


def prepare(pieces, where, scale):
    n = len(pieces)
    groups, halves, rows, tokens = pieces[0].shape
    whole = pl.BlockSpec((groups, halves, rows, tokens), lambda k, w: (0, 0, 0, 0))
    return pl.pallas_call(
        functools.partial(prepare_kernel, n),
        grid_spec=pltpu.PrefetchScalarGridSpec(
            num_scalar_prefetch=1,
            grid=(n,),
            in_specs=[pl.BlockSpec((groups, tokens), lambda k, w: (0, 0))] + [whole] * n,
            out_specs=pl.BlockSpec(
                (groups, halves, 1, rows, tokens), lambda k, w: (0, 0, w[k], 0, 0)
            ),
        ),
        out_shape=jax.ShapeDtypeStruct((groups, halves, n, rows, tokens), BF16),
        cost_estimate=pl.CostEstimate(
            flops=groups * halves * n * rows * tokens,
            bytes_accessed=4 * groups * halves * n * rows * tokens,
            transcendentals=0,
        ),
        compiler_params=pltpu.CompilerParams(vmem_limit_bytes=VMEM_LIMIT),
        name="prepare",
    )(where, scale, *pieces)


def on_device(n_dp, n_tensor, hidden_act, out_grad, other_sq):
    examples = other_sq.shape[0]
    tokens, columns = hidden_act.shape
    features = out_grad.shape[1]
    length = tokens // examples
    chips = n_tensor // 2
    me = lax.axis_index("dp")
    place = lax.axis_index("tensor")

    near = [1 << i for i in range(n_dp.bit_length() - 1)]
    spans = cut(columns, NEAR_SHARES)
    parts, held = [], hidden_act
    for start, width in spans:
        parts.append(lax.slice_in_dim(held, start, start + width, axis=1))
        held = after(held, parts[-1])[0]
    blocks = {mask: [swap(parts[0], "dp", n_dp, mask)] for mask in near}

    grad = out_grad.T
    share = features // n_tensor
    spread = lax.all_to_all(grad.reshape(n_tensor, share, tokens), "tensor", split_axis=0, concat_axis=0, tiled=True)
    halves = n_tensor // n_dp
    spread = spread.reshape(n_dp, halves, share, tokens)
    mine = [
        lax.dynamic_index_in_dim(spread, me ^ s, 0, keepdims=False) for s in range(n_dp)
    ]
    exchanged = [swap(mine[s], "dp", n_dp, s) for s in range(1, n_dp)]
    for p in range(1, len(spans)):
        for mask in near:
            blocks[mask].append(swap(parts[p], "dp", n_dp, mask))
    piece = jnp.stack([mine[0]] + exchanged)

    acts = hidden_act.reshape(examples, length, columns)
    act_gram = jnp.einsum("etf,esf->ets", acts, acts, preferred_element_type=F32)
    grads = grad.reshape(features, examples, length)
    grad_gram = jnp.einsum("fet,fes->ets", grads, grads, preferred_element_type=F32)
    grams = jnp.stack([act_gram.reshape(tokens, length), grad_gram.reshape(tokens, length)])
    rows, first = tokens, 0
    mask = 1
    while mask < n_tensor:
        rows //= 2
        bit = (place // mask) % 2
        sent = lax.dynamic_slice_in_dim(grams, (1 - bit) * rows, rows, 1)
        kept = lax.dynamic_slice_in_dim(grams, bit * rows, rows, 1)
        grams = kept + swap(sent, "tensor", n_tensor, mask)
        first = first + bit * rows
        mask *= 2
    row_sum = jnp.sum(grams[0] * grams[1], axis=1)
    example = (first + jnp.arange(rows, dtype=jnp.int32)) // length
    layer_sq = jnp.sum(
        jnp.where(example[None] == jnp.arange(examples, dtype=jnp.int32)[:, None], row_sum[None], 0.0),
        axis=1,
    )
    mask = 1
    while mask < n_tensor:
        layer_sq = layer_sq + swap(layer_sq, "tensor", n_tensor, mask)
        mask *= 2
    total_columns, total_features = columns * n_tensor, features * n_tensor
    clip_bound = math.sqrt(length * total_columns * total_features / CLIP_DIVISOR)
    clip_scale = jnp.minimum(1.0, clip_bound / jnp.sqrt(other_sq + layer_sq))
    ring = [(i, (i + 2) % n_tensor) for i in range(n_tensor)]
    piece, clip_scale = after(piece, clip_scale)
    pieces, where = [], []
    for k in range(chips):
        if k:
            piece = lax.ppermute(piece, "tensor", ring)
        origin = (place // 2 - k) % chips * 2
        pieces += [piece, swap(piece, "tensor", n_tensor, 1)]
        where += [origin + place % 2, origin + (place + 1) % 2]
    scales = jnp.stack([clip_scale] + [swap(clip_scale, "dp", n_dp, s) for s in range(1, n_dp)])
    token_scale = jnp.broadcast_to(scales[:, :, None], (n_dp, examples, length)).reshape(n_dp, tokens)
    scaled = prepare(pieces, jnp.stack(where).astype(jnp.int32), token_scale)
    scaled = scaled.reshape(n_dp, halves * n_tensor * share, tokens)

    def own_or_near(start):
        p = max(i for i, (first, _) in enumerate(spans) if first <= start)
        return {0: (hidden_act, start), **{m: (blocks[m][p], start - spans[p][0]) for m in near}}

    chunks = cut(columns, CHUNK_SHARES)
    out_shape = (scaled.shape[1], columns)
    ahead = [c for c, (start, _) in enumerate(chunks) if start >= spans[-1][0]] if len(spans) > 1 else []
    ahead = ahead if n_dp > 2 else []
    out = None
    if ahead:
        first = chunks[ahead[0]][0]
        out = chunk_matmul(scaled, own_or_near(first), out, first, columns - first, False, out_shape)
    for c, (start, width) in enumerate(chunks):
        half = width // 2
        known = own_or_near(start)
        halves_of = {}
        for side in (0, 1):
            for mask, (array, at) in known.items():
                halves_of[mask, side] = (array, at + side * half)
        far = sorted((m for m in range(n_dp) if m not in known), key=lambda m: len(bits_of(m)))
        acts = {}
        for mask in far:
            bits = bits_of(mask)
            for side in (0, 1):
                bit = bits[(2 * c + side) % len(bits)]
                source, at = halves_of[mask ^ bit, side]
                if source.shape[1] != half:
                    source = lax.slice_in_dim(source, at, at + half, axis=1)
                halves_of[mask, side] = (swap(source, "dp", n_dp, bit), 0)
            acts[mask] = (halves_of[mask, 0][0], halves_of[mask, 1][0])
        if c not in ahead:
            acts = {**known, **acts}
        out = chunk_matmul(scaled, acts, out, start, width, c in ahead, out_shape)
    return out


def solution(mesh):
    placed = (P("dp", "tensor"), P("dp", "tensor"), P("dp"))

    def body(hidden_act, out_grad, other_sq):
        return on_device(
            mesh.shape["dp"], mesh.shape["tensor"], hidden_act, out_grad, other_sq
        )

    return jax.shard_map(
        body, mesh=mesh, in_specs=placed, out_specs=P("dp", "tensor"), check_vma=False
    )
```

```python
import functools
import math

import jax
import jax.numpy as jnp
from jax import lax
from jax.experimental import pallas as pl
from jax.experimental.pallas import tpu as pltpu
from jax.sharding import PartitionSpec as P


BF16, F32 = jnp.bfloat16, jnp.float32
CLIP_DIVISOR = 80.0
VMEM_LIMIT = 51 << 20
NEAR_SHARES = (2, 3, 2, 2)
CHUNK_SHARES = (2, 3, 2, 1, 1)


def bits_of(mask):
    return [1 << i for i in range(mask.bit_length()) if mask >> i & 1]


def swap(x, axis, size, mask):
    return lax.ppermute(x, axis, [(i, i ^ mask) for i in range(size)])


def after(*arrays):
    return lax.optimization_barrier(arrays)


def cut(total, shares):
    if total % (2 * sum(shares)):
        shares = (1,)
    unit, start, pieces = total // sum(shares), 0, []
    for share in shares:
        pieces.append((start, share * unit))
        start += share * unit
    return pieces


def row_block(rows):
    for block in (288, 192, 144, 128, 96, 64, 48, 32, 16, 8):
        if rows % block == 0:
            return block
    return rows


def matmul_kernel(terms, block, tiles, adds, *refs):
    grad_ref, out_ref, refs = refs[0], refs[-1], refs[1:]

    def multiply(side):
        for at in range(0, out_ref.shape[0], block):
            here = pl.ds(at, block)
            total, k = (refs[-2][here, :] if adds else None), 0
            for s, arrays in terms:
                act_ref = refs[k + side % arrays]
                k += arrays
                product = jnp.dot(grad_ref[s, here, :], act_ref[...], preferred_element_type=F32)
                total = product if total is None else total + product
            out_ref[here, :] = total

    if any(arrays > 1 for _, arrays in terms):
        step = pl.program_id(0)
        pl.when(step < tiles)(lambda: multiply(0))
        pl.when(step >= tiles)(lambda: multiply(1))
    else:
        multiply(0)


def chunk_matmul(grads, acts, out, start, width, adds, out_shape, to=None):
    _, rows, tokens = grads.shape
    tile = math.gcd(width // 2, 256)
    tiles = width // 2 // tile
    specs, args, terms = [pl.BlockSpec(memory_space=pltpu.VMEM)], [grads], []
    args = [pltpu.with_memory_space_constraint(grads, pltpu.VMEM)]
    for s, (array, other) in acts.items():
        if isinstance(other, int):
            maps = [(array, lambda j, at=other // tile: (0, at + j))]
        else:
            maps = [
                (array, lambda j: (0, jnp.minimum(j, tiles - 1))),
                (other, lambda j: (0, jnp.maximum(j - tiles, 0))),
            ]
        for array, index in maps:
            args.append(array)
            specs.append(pl.BlockSpec((tokens, tile), index))
        terms.append((s, len(maps)))
    first = (start if to is None else to) // tile
    window = pl.BlockSpec((rows, tile), lambda j: (0, first + j))
    aliases = {}
    if out is not None:
        specs.append(window if adds else pl.BlockSpec(memory_space=pl.ANY))
        args.append(out)
        aliases = {len(args) - 1: 0}
    return pl.pallas_call(
        functools.partial(matmul_kernel, terms, row_block(rows), tiles, adds),
        grid=(2 * tiles,),
        in_specs=specs,
        out_specs=window,
        out_shape=jax.ShapeDtypeStruct(out_shape, F32),
        input_output_aliases=aliases,
        compiler_params=pltpu.CompilerParams(vmem_limit_bytes=VMEM_LIMIT),
        cost_estimate=pl.CostEstimate(
            flops=2 * rows * width * len(terms) * tokens,
            bytes_accessed=2 * len(terms) * tokens * width + 4 * rows * width * (1 + adds),
            transcendentals=0,
        ),
    )(*args)


def finish_kernel(terms, block, *refs):
    grad_ref, known_ref, out_ref, act_refs = refs[0], refs[1], refs[-1], refs[2:]
    here = pl.ds(pl.multiple_of(pl.program_id(0) * block, block), block)
    half = out_ref.shape[1] // 2
    for side in (0, 1):
        columns = pl.ds(side * half, half)
        total = known_ref[here, columns]
        for k, s in enumerate(terms):
            total += jnp.dot(grad_ref[s, here, :], act_refs[2 * k + side][...], preferred_element_type=F32)
        out_ref[:, columns] = total


def finish_chunk(grads, known, acts, out, start, width):
    _, rows, tokens = grads.shape
    block = rows // 2
    args = [grads, known] + [half for halves in acts.values() for half in halves]
    args = [pltpu.with_memory_space_constraint(a, pltpu.VMEM) for a in args]
    specs = [pl.BlockSpec(memory_space=pltpu.VMEM)] * len(args)
    return pl.pallas_call(
        functools.partial(finish_kernel, tuple(acts), block),
        grid=(rows // block,),
        in_specs=specs + [pl.BlockSpec(memory_space=pl.ANY)],
        out_specs=pl.BlockSpec((block, width), lambda i: (i, start // width)),
        out_shape=jax.ShapeDtypeStruct(out.shape, F32),
        input_output_aliases={len(args): 0},
        compiler_params=pltpu.CompilerParams(vmem_limit_bytes=VMEM_LIMIT),
        cost_estimate=pl.CostEstimate(
            flops=2 * rows * width * len(acts) * tokens, bytes_accessed=4 * rows * width, transcendentals=0
        ),
        name="finish",
    )(*args, out)


def prepare_kernel(n, where_ref, scale_ref, *refs):
    pieces, out_ref = refs[:n], refs[n]
    step = pl.program_id(0)
    scale = scale_ref[...]
    for k in range(n):

        @pl.when(step == k)
        def _(k=k):
            piece = pieces[k][...]
            out_ref[...] = (piece.astype(F32) * scale[:, None, None, :]).astype(BF16)[:, :, None]


def prepare(pieces, where, scale):
    n = len(pieces)
    groups, halves, rows, tokens = pieces[0].shape
    whole = pl.BlockSpec((groups, halves, rows, tokens), lambda k, w: (0, 0, 0, 0))
    return pl.pallas_call(
        functools.partial(prepare_kernel, n),
        grid_spec=pltpu.PrefetchScalarGridSpec(
            num_scalar_prefetch=1,
            grid=(n,),
            in_specs=[pl.BlockSpec((groups, tokens), lambda k, w: (0, 0))] + [whole] * n,
            out_specs=pl.BlockSpec(
                (groups, halves, 1, rows, tokens), lambda k, w: (0, 0, w[k], 0, 0)
            ),
        ),
        out_shape=jax.ShapeDtypeStruct((groups, halves, n, rows, tokens), BF16),
        cost_estimate=pl.CostEstimate(
            flops=groups * halves * n * rows * tokens,
            bytes_accessed=4 * groups * halves * n * rows * tokens,
            transcendentals=0,
        ),
        compiler_params=pltpu.CompilerParams(vmem_limit_bytes=VMEM_LIMIT),
        name="prepare",
    )(where, scale, *pieces)


def on_device(n_dp, n_tensor, hidden_act, out_grad, other_sq):
    examples = other_sq.shape[0]
    tokens, columns = hidden_act.shape
    features = out_grad.shape[1]
    length = tokens // examples
    chips = n_tensor // 2
    me = lax.axis_index("dp")
    place = lax.axis_index("tensor")

    near = [1 << i for i in range(n_dp.bit_length() - 1)]
    spans = cut(columns, NEAR_SHARES)
    parts, held = [], hidden_act
    for start, width in spans:
        parts.append(lax.slice_in_dim(held, start, start + width, axis=1))
        held = after(held, parts[-1])[0]
    blocks = {mask: [swap(parts[0], "dp", n_dp, mask)] for mask in near}

    grad = out_grad.T
    share = features // n_tensor
    spread = lax.all_to_all(grad.reshape(n_tensor, share, tokens), "tensor", split_axis=0, concat_axis=0, tiled=True)
    halves = n_tensor // n_dp
    spread = spread.reshape(n_dp, halves, share, tokens)
    mine = [
        lax.dynamic_index_in_dim(spread, me ^ s, 0, keepdims=False) for s in range(n_dp)
    ]
    exchanged = [swap(mine[s], "dp", n_dp, s) for s in range(1, n_dp)]
    for p in range(1, len(spans)):
        for mask in near:
            blocks[mask].append(swap(parts[p], "dp", n_dp, mask))
    piece = jnp.stack([mine[0]] + exchanged)

    acts = hidden_act.reshape(examples, length, columns)
    act_gram = jnp.einsum("etf,esf->ets", acts, acts, preferred_element_type=F32)
    grads = grad.reshape(features, examples, length)
    grad_gram = jnp.einsum("fet,fes->ets", grads, grads, preferred_element_type=F32)
    grams = jnp.stack([act_gram.reshape(tokens, length), grad_gram.reshape(tokens, length)])
    rows, first = tokens, 0
    mask = 1
    while mask < n_tensor:
        rows //= 2
        bit = (place // mask) % 2
        sent = lax.dynamic_slice_in_dim(grams, (1 - bit) * rows, rows, 1)
        kept = lax.dynamic_slice_in_dim(grams, bit * rows, rows, 1)
        grams = kept + swap(sent, "tensor", n_tensor, mask)
        first = first + bit * rows
        mask *= 2
    row_sum = jnp.sum(grams[0] * grams[1], axis=1)
    example = (first + jnp.arange(rows, dtype=jnp.int32)) // length
    layer_sq = jnp.sum(
        jnp.where(example[None] == jnp.arange(examples, dtype=jnp.int32)[:, None], row_sum[None], 0.0),
        axis=1,
    )
    mask = 1
    while mask < n_tensor:
        layer_sq = layer_sq + swap(layer_sq, "tensor", n_tensor, mask)
        mask *= 2
    total_columns, total_features = columns * n_tensor, features * n_tensor
    clip_bound = math.sqrt(length * total_columns * total_features / CLIP_DIVISOR)
    clip_scale = jnp.minimum(1.0, clip_bound / jnp.sqrt(other_sq + layer_sq))
    ring = [(i, (i + 2) % n_tensor) for i in range(n_tensor)]
    piece, clip_scale = after(piece, clip_scale)
    pieces, where = [], []
    for k in range(chips):
        if k:
            piece = lax.ppermute(piece, "tensor", ring)
        origin = (place // 2 - k) % chips * 2
        pieces += [piece, swap(piece, "tensor", n_tensor, 1)]
        where += [origin + place % 2, origin + (place + 1) % 2]
    scales = jnp.stack([clip_scale] + [swap(clip_scale, "dp", n_dp, s) for s in range(1, n_dp)])
    token_scale = jnp.broadcast_to(scales[:, :, None], (n_dp, examples, length)).reshape(n_dp, tokens)
    scaled = prepare(pieces, jnp.stack(where).astype(jnp.int32), token_scale)
    scaled = scaled.reshape(n_dp, halves * n_tensor * share, tokens)

    def own_or_near(start):
        p = max(i for i, (first, _) in enumerate(spans) if first <= start)
        return {0: (hidden_act, start), **{m: (blocks[m][p], start - spans[p][0]) for m in near}}

    chunks = cut(columns, CHUNK_SHARES)
    out_shape = (scaled.shape[1], columns)
    ahead = [c for c, (start, _) in enumerate(chunks) if start >= spans[-1][0]] if len(spans) > 1 else []
    ahead = ahead if n_dp > 2 else []
    out = None
    known_sums = {}
    for c in ahead:
        start, width = chunks[c]
        known_sums[c] = chunk_matmul(scaled, own_or_near(start), None, start, width, False, (out_shape[0], width), 0)
    for c, (start, width) in enumerate(chunks):
        half = width // 2
        known = own_or_near(start)
        halves_of = {}
        for side in (0, 1):
            for mask, (array, at) in known.items():
                halves_of[mask, side] = (array, at + side * half)
        far = sorted((m for m in range(n_dp) if m not in known), key=lambda m: len(bits_of(m)))
        acts = {}
        for mask in far:
            bits = bits_of(mask)
            for side in (0, 1):
                bit = bits[(2 * c + side) % len(bits)]
                source, at = halves_of[mask ^ bit, side]
                if source.shape[1] != half:
                    source = lax.slice_in_dim(source, at, at + half, axis=1)
                halves_of[mask, side] = (swap(source, "dp", n_dp, bit), 0)
            acts[mask] = (halves_of[mask, 0][0], halves_of[mask, 1][0])
        if c in ahead:
            out = finish_chunk(scaled, known_sums[c], acts, out, start, width)
        else:
            out = chunk_matmul(scaled, {**known, **acts}, out, start, width, False, out_shape)
    return out


def solution(mesh):
    placed = (P("dp", "tensor"), P("dp", "tensor"), P("dp"))

    def body(hidden_act, out_grad, other_sq):
        return on_device(
            mesh.shape["dp"], mesh.shape["tensor"], hidden_act, out_grad, other_sq
        )

    return jax.shard_map(
        body, mesh=mesh, in_specs=placed, out_specs=P("dp", "tensor"), check_vma=False
    )
```

```python
import functools
import math

import jax
import jax.numpy as jnp
from jax import lax
from jax.experimental import pallas as pl
from jax.experimental.pallas import tpu as pltpu
from jax.sharding import PartitionSpec as P


BF16, F32 = jnp.bfloat16, jnp.float32
CLIP_DIVISOR = 80.0
VMEM_LIMIT = 51 << 20
NEAR_SHARES = (2, 3, 2, 2)
CHUNK_SHARES = (2, 3, 2, 1, 1)


def bits_of(mask):
    return [1 << i for i in range(mask.bit_length()) if mask >> i & 1]


def swap(x, axis, size, mask):
    return lax.ppermute(x, axis, [(i, i ^ mask) for i in range(size)])


def after(*arrays):
    return lax.optimization_barrier(arrays)


def cut(total, shares):
    if total % (2 * sum(shares)):
        shares = (1,)
    unit, start, pieces = total // sum(shares), 0, []
    for share in shares:
        pieces.append((start, share * unit))
        start += share * unit
    return pieces


def row_block(rows):
    for block in (288, 192, 144, 128, 96, 64, 48, 32, 16, 8):
        if rows % block == 0:
            return block
    return rows


def matmul_kernel(terms, block, tiles, adds, *refs):
    grad_ref, out_ref, refs = refs[0], refs[-1], refs[1:]

    def multiply(side):
        for at in range(0, out_ref.shape[0], block):
            here = pl.ds(at, block)
            total, k = (refs[-2][here, :] if adds else None), 0
            for s, arrays in terms:
                act_ref = refs[k + side % arrays]
                k += arrays
                product = jnp.dot(grad_ref[s, here, :], act_ref[...], preferred_element_type=F32)
                total = product if total is None else total + product
            out_ref[here, :] = total

    if any(arrays > 1 for _, arrays in terms):
        step = pl.program_id(0)
        pl.when(step < tiles)(lambda: multiply(0))
        pl.when(step >= tiles)(lambda: multiply(1))
    else:
        multiply(0)


def chunk_matmul(grads, acts, out, start, width, adds, out_shape, to=None):
    _, rows, tokens = grads.shape
    tile = math.gcd(width // 2, 256)
    tiles = width // 2 // tile
    specs, args, terms = [pl.BlockSpec(memory_space=pltpu.VMEM)], [grads], []
    args = [pltpu.with_memory_space_constraint(grads, pltpu.VMEM)]
    for s, (array, other) in acts.items():
        if isinstance(other, int):
            maps = [(array, lambda j, at=other // tile: (0, at + j))]
        else:
            maps = [
                (array, lambda j: (0, jnp.minimum(j, tiles - 1))),
                (other, lambda j: (0, jnp.maximum(j - tiles, 0))),
            ]
        for array, index in maps:
            args.append(array)
            specs.append(pl.BlockSpec((tokens, tile), index))
        terms.append((s, len(maps)))
    first = (start if to is None else to) // tile
    window = pl.BlockSpec((rows, tile), lambda j: (0, first + j))
    aliases = {}
    if out is not None:
        specs.append(window if adds else pl.BlockSpec(memory_space=pl.ANY))
        args.append(out)
        aliases = {len(args) - 1: 0}
    return pl.pallas_call(
        functools.partial(matmul_kernel, terms, row_block(rows), tiles, adds),
        grid=(2 * tiles,),
        in_specs=specs,
        out_specs=window,
        out_shape=jax.ShapeDtypeStruct(out_shape, F32),
        input_output_aliases=aliases,
        compiler_params=pltpu.CompilerParams(vmem_limit_bytes=VMEM_LIMIT),
        cost_estimate=pl.CostEstimate(
            flops=2 * rows * width * len(terms) * tokens,
            bytes_accessed=2 * len(terms) * tokens * width + 4 * rows * width * (1 + adds),
            transcendentals=0,
        ),
    )(*args)


def first_columns_kernel(in_ref, out_ref, sems):
    columns = pl.ds(0, out_ref.shape[1])
    block = in_ref.shape[0] // sems.shape[0]
    copies = []
    for i in range(sems.shape[0]):
        rows = pl.ds(i * block, block)
        copies.append(pltpu.make_async_copy(in_ref.at[rows, columns], out_ref.at[rows, :], sems.at[i]))
    for copy in copies:
        copy.start()
    for copy in copies:
        copy.wait()


def first_columns(array, width):
    rows = array.shape[0]
    return pl.pallas_call(
        first_columns_kernel,
        in_specs=[pl.BlockSpec(memory_space=pltpu.HBM)],
        out_specs=pl.BlockSpec(memory_space=pltpu.VMEM),
        out_shape=pltpu.VMEM((rows, width), array.dtype),
        compiler_params=pltpu.CompilerParams(vmem_limit_bytes=8 << 20),
        scratch_shapes=[pltpu.SemaphoreType.DMA((4 if rows % 64 == 0 else 1,))],
        name="first_columns",
    )(pltpu.with_memory_space_constraint(array, pltpu.HBM))


def finish_kernel(terms, block, *refs):
    grad_ref, known_ref, out_ref, act_refs = refs[0], refs[1], refs[-1], refs[2:]
    here = pl.ds(pl.multiple_of(pl.program_id(0) * block, block), block)
    half = out_ref.shape[1] // 2
    for side in (0, 1):
        columns = pl.ds(side * half, half)
        total = known_ref[here, columns]
        for k, s in enumerate(terms):
            total += jnp.dot(grad_ref[s, here, :], act_refs[2 * k + side][...], preferred_element_type=F32)
        out_ref[:, columns] = total


def finish_chunk(grads, known, acts, out, start, width):
    _, rows, tokens = grads.shape
    block = rows // 2
    args = [grads, known] + [half for halves in acts.values() for half in halves]
    args = [pltpu.with_memory_space_constraint(a, pltpu.VMEM) for a in args]
    specs = [pl.BlockSpec(memory_space=pltpu.VMEM)] * len(args)
    return pl.pallas_call(
        functools.partial(finish_kernel, tuple(acts), block),
        grid=(rows // block,),
        in_specs=specs + [pl.BlockSpec(memory_space=pl.ANY)],
        out_specs=pl.BlockSpec((block, width), lambda i: (i, start // width)),
        out_shape=jax.ShapeDtypeStruct(out.shape, F32),
        input_output_aliases={len(args): 0},
        compiler_params=pltpu.CompilerParams(vmem_limit_bytes=VMEM_LIMIT),
        cost_estimate=pl.CostEstimate(
            flops=2 * rows * width * len(acts) * tokens, bytes_accessed=4 * rows * width, transcendentals=0
        ),
        name="finish",
    )(*args, out)


def prepare_kernel(n, where_ref, scale_ref, *refs):
    pieces, out_ref = refs[:n], refs[n]
    step = pl.program_id(0)
    scale = scale_ref[...]
    for k in range(n):

        @pl.when(step == k)
        def _(k=k):
            piece = pieces[k][...]
            out_ref[...] = (piece.astype(F32) * scale[:, None, None, :]).astype(BF16)[:, :, None]


def prepare(pieces, where, scale):
    n = len(pieces)
    groups, halves, rows, tokens = pieces[0].shape
    whole = pl.BlockSpec((groups, halves, rows, tokens), lambda k, w: (0, 0, 0, 0))
    return pl.pallas_call(
        functools.partial(prepare_kernel, n),
        grid_spec=pltpu.PrefetchScalarGridSpec(
            num_scalar_prefetch=1,
            grid=(n,),
            in_specs=[pl.BlockSpec((groups, tokens), lambda k, w: (0, 0))] + [whole] * n,
            out_specs=pl.BlockSpec(
                (groups, halves, 1, rows, tokens), lambda k, w: (0, 0, w[k], 0, 0)
            ),
        ),
        out_shape=jax.ShapeDtypeStruct((groups, halves, n, rows, tokens), BF16),
        cost_estimate=pl.CostEstimate(
            flops=groups * halves * n * rows * tokens,
            bytes_accessed=4 * groups * halves * n * rows * tokens,
            transcendentals=0,
        ),
        compiler_params=pltpu.CompilerParams(vmem_limit_bytes=VMEM_LIMIT),
        name="prepare",
    )(where, scale, *pieces)


def on_device(n_dp, n_tensor, hidden_act, out_grad, other_sq):
    examples = other_sq.shape[0]
    tokens, columns = hidden_act.shape
    features = out_grad.shape[1]
    length = tokens // examples
    chips = n_tensor // 2
    me = lax.axis_index("dp")
    place = lax.axis_index("tensor")

    near = [1 << i for i in range(n_dp.bit_length() - 1)]
    spans = cut(columns, NEAR_SHARES)
    parts, held = [], hidden_act
    for start, width in spans:
        if start == 0:
            parts.append(first_columns(held, width))
        else:
            parts.append(lax.slice_in_dim(held, start, start + width, axis=1))
        held = after(held, parts[-1])[0]
    blocks = {mask: [swap(parts[0], "dp", n_dp, mask)] for mask in near}

    grad = out_grad.T
    share = features // n_tensor
    spread = lax.all_to_all(grad.reshape(n_tensor, share, tokens), "tensor", split_axis=0, concat_axis=0, tiled=True)
    halves = n_tensor // n_dp
    spread = spread.reshape(n_dp, halves, share, tokens)
    mine = [
        lax.dynamic_index_in_dim(spread, me ^ s, 0, keepdims=False) for s in range(n_dp)
    ]
    exchanged = [swap(mine[s], "dp", n_dp, s) for s in range(1, n_dp)]
    for p in range(1, len(spans)):
        for mask in near:
            blocks[mask].append(swap(parts[p], "dp", n_dp, mask))
    piece = jnp.stack([mine[0]] + exchanged)

    acts = hidden_act.reshape(examples, length, columns)
    act_gram = jnp.einsum("etf,esf->ets", acts, acts, preferred_element_type=F32)
    grads = grad.reshape(features, examples, length)
    grad_gram = jnp.einsum("fet,fes->ets", grads, grads, preferred_element_type=F32)
    grams = jnp.stack([act_gram.reshape(tokens, length), grad_gram.reshape(tokens, length)])
    rows, first = tokens, 0
    mask = 1
    while mask < n_tensor:
        rows //= 2
        bit = (place // mask) % 2
        sent = lax.dynamic_slice_in_dim(grams, (1 - bit) * rows, rows, 1)
        kept = lax.dynamic_slice_in_dim(grams, bit * rows, rows, 1)
        grams = kept + swap(sent, "tensor", n_tensor, mask)
        first = first + bit * rows
        mask *= 2
    row_sum = jnp.sum(grams[0] * grams[1], axis=1)
    example = (first + jnp.arange(rows, dtype=jnp.int32)) // length
    layer_sq = jnp.sum(
        jnp.where(example[None] == jnp.arange(examples, dtype=jnp.int32)[:, None], row_sum[None], 0.0),
        axis=1,
    )
    mask = 1
    while mask < n_tensor:
        layer_sq = layer_sq + swap(layer_sq, "tensor", n_tensor, mask)
        mask *= 2
    total_columns, total_features = columns * n_tensor, features * n_tensor
    clip_bound = math.sqrt(length * total_columns * total_features / CLIP_DIVISOR)
    clip_scale = jnp.minimum(1.0, clip_bound / jnp.sqrt(other_sq + layer_sq))
    ring = [(i, (i + 2) % n_tensor) for i in range(n_tensor)]
    piece, clip_scale = after(piece, clip_scale)
    pieces, where = [], []
    for k in range(chips):
        if k:
            piece = lax.ppermute(piece, "tensor", ring)
        origin = (place // 2 - k) % chips * 2
        pieces += [piece, swap(piece, "tensor", n_tensor, 1)]
        where += [origin + place % 2, origin + (place + 1) % 2]
    scales = jnp.stack([clip_scale] + [swap(clip_scale, "dp", n_dp, s) for s in range(1, n_dp)])
    token_scale = jnp.broadcast_to(scales[:, :, None], (n_dp, examples, length)).reshape(n_dp, tokens)
    scaled = prepare(pieces, jnp.stack(where).astype(jnp.int32), token_scale)
    scaled = scaled.reshape(n_dp, halves * n_tensor * share, tokens)

    def own_or_near(start):
        p = max(i for i, (first, _) in enumerate(spans) if first <= start)
        return {0: (hidden_act, start), **{m: (blocks[m][p], start - spans[p][0]) for m in near}}

    chunks = cut(columns, CHUNK_SHARES)
    out_shape = (scaled.shape[1], columns)
    ahead = [c for c, (start, _) in enumerate(chunks) if start >= spans[-1][0]] if len(spans) > 1 else []
    ahead = ahead if n_dp > 2 else []
    out = None
    known_sums = {}
    for c in ahead:
        start, width = chunks[c]
        known_sums[c] = chunk_matmul(scaled, own_or_near(start), None, start, width, False, (out_shape[0], width), 0)
    for c, (start, width) in enumerate(chunks):
        half = width // 2
        known = own_or_near(start)
        halves_of = {}
        for side in (0, 1):
            for mask, (array, at) in known.items():
                halves_of[mask, side] = (array, at + side * half)
        far = sorted((m for m in range(n_dp) if m not in known), key=lambda m: len(bits_of(m)))
        acts = {}
        for mask in far:
            bits = bits_of(mask)
            for side in (0, 1):
                bit = bits[(2 * c + side) % len(bits)]
                source, at = halves_of[mask ^ bit, side]
                if source.shape[1] != half:
                    source = lax.slice_in_dim(source, at, at + half, axis=1)
                halves_of[mask, side] = (swap(source, "dp", n_dp, bit), 0)
            acts[mask] = (halves_of[mask, 0][0], halves_of[mask, 1][0])
        if c in ahead:
            out = finish_chunk(scaled, known_sums[c], acts, out, start, width)
        else:
            out = chunk_matmul(scaled, {**known, **acts}, out, start, width, False, out_shape)
    return out


def solution(mesh):
    placed = (P("dp", "tensor"), P("dp", "tensor"), P("dp"))

    def body(hidden_act, out_grad, other_sq):
        return on_device(
            mesh.shape["dp"], mesh.shape["tensor"], hidden_act, out_grad, other_sq
        )

    return jax.shard_map(
        body, mesh=mesh, in_specs=placed, out_specs=P("dp", "tensor"), check_vma=False
    )
```
